512 devices in a mesh: pts: 32 (over z, x), comp: 16 (over y, core).
Axes of the slice: x: 4, y: 8, z: 8, core: 2. Of those that a mesh axis runs over, the one named last changes fastest.
Arguments:
- points: bfloat16 [65536, 3072], P(('pts', 'comp')), may hold values from -6 to 6
- candidates: int32 [65536, 4], P(('pts', 'comp')), may hold values from 0 to 31, all different within a row; in each aligned block of 128 rows (0 to 127, 128 to 255, ...) at most 32 rows name the same one
- means: bfloat16 [4096, 3072], P('comp'), may hold values from -0.75 to 0.75
- variances: float32 [4096], P('comp'), may hold values from 0.9 to 1.1
- log_weights: float32 [4096], P('comp'), may hold values from -4 to 4
Outputs:
- loglik: float32 [65536], P(('pts', 'comp'))
- new_means: float32 [16, 256, 3072], P('comp', 'pts')
- new_variances: float32 [16, 256], P('comp', 'pts')
- new_log_weights: float32 [16, 256], P('comp', 'pts')
The draws below stay inside these ranges and needn't reach their ends.
Inputs may be any that keep to these rules, and one draw needn't show every extreme that they name: `candidates`: each row names 4 different blocks. Among the 128 rows of one device, no block is named by more than 32 rows, and some block is named by exactly 32 rows.
All inputs are finite; a program needn't handle non-finite values.
Results may differ from the reference program's by a relative error of at most 0.0065.
Values may be sent and summed in bfloat16 or wider, within the bound.
No kernel may reach another device: no remote copies, remote signals or barrier semaphores. Data moves between devices by JAX's collectives and lax.ppermute only.
A program may use at most 64 MiB of HBM per device.

```python
import math
import jax
import jax.numpy as jnp
import numpy as np
from jax import lax

D = 3072
BLOCK = 128
CANDS = 4
PTS_DEV = 128
KDEV = 256
K = 4096
NBLK = 32
CAP = 32
NPTS = 65536
N_PTS = 32
N_COMP = 16


def shard_levels(stream_key, extent, pieces, smallest, top_value):
    gain, own = 1.0, jax.random.fold_in(stream_key, 6)
    for position, shards_of in pieces:
        heights = jnp.exp(jax.random.uniform(jax.random.fold_in(own, position), (shards_of,), jnp.float32, smallest / len(pieces), top_value / len(pieces)))
        gain = gain * jnp.repeat(heights, extent[position] // shards_of).reshape([-1 if axis == position else 1 for axis in range(len(extent))])
    return gain


def deal_out(key, own, number, rows, number_of, top, reach, lean):
    order = jax.random.permutation(key, number_of)
    heavy_load, usual = portions_of(number_of, rows * top, reach, lean, True), portions_of(number_of, rows * top, reach, lean, False)
    places = jnp.arange(number_of)

    def named(lengths, turn):
        used = int((lengths > 0).sum())
        fixed = max(1, used // 4)
        moved = fixed + (places - fixed + turn * (used - fixed)) % max(1, number_of - fixed)
        return jnp.zeros((number_of,), jnp.int32).at[order[jnp.where(places < fixed, places, moved)]].set(jnp.asarray(lengths, jnp.int32))

    lengths = jnp.where(number % 4 == 0, named(heavy_load, number // 4), named(usual, number - number // 4 - 1))
    mixed = jax.random.permutation(jax.random.fold_in(own, 3), number_of)
    donor, sink = mixed[0:number_of // 2 * 2:2], mixed[1:number_of // 2 * 2:2]
    margin = jnp.minimum(lengths[donor] - 1, reach - lengths[sink]) // 2
    margin = jnp.where((donor == order[0]) | (sink == order[0]) | (lengths[sink] == 0), 0, jnp.maximum(margin, 0))
    moved = jax.random.randint(jax.random.fold_in(own, 4), (number_of // 2,), 0, 1 << 20) % (margin + 1)
    lengths = lengths.at[donor].add(-moved).at[sink].add(moved)
    members = jnp.searchsorted(jnp.cumsum(lengths), jnp.arange(rows * top), side="right").astype(jnp.int32)
    listing = members.reshape(top, rows).T
    listing = listing[jax.random.permutation(jax.random.fold_in(own, 1), rows)]
    turn = jax.random.randint(jax.random.fold_in(own, 2), (rows, 1), 0, top)
    return jnp.take_along_axis(listing, (jnp.arange(top)[None, :] + turn) % top, axis=1)


def portions_of(count, total, bound, lean, full):
    weights = [(1 << 20) // math.isqrt(standing ** lean) + 1 for standing in range(1, count + 1)]
    largest = bound if full else min(bound, max(-(-total // count), total * weights[0] // sum(weights)))
    least = 1 if total - largest >= count - 1 else 0
    given, surplus = [largest] + [least] * (count - 1), total - largest - least * (count - 1)
    while surplus > 0:
        movable = [i for i in range(1, count) if given[i] < largest] or [i for i in range(1, count) if given[i] < bound]
        whole, left = sum([weights[i] for i in movable]), surplus
        for i in movable:
            addition = min(bound - given[i], max(1, left * weights[i] // whole), surplus)
            given[i] = given[i] + addition
            surplus = surplus - addition
    return np.array(given)


def scatter_about(stream_key, dims, deviation, limit, pieces=(), held_as=jnp.bfloat16):
    result = deviation * jax.random.normal(stream_key, dims, jnp.float32)
    if pieces:
        result = result * shard_levels(stream_key, dims, pieces, -0.22, 0.18)
    return jnp.clip(result, -limit, limit).astype(held_as)


def setup_inputs(seed: int = 0) -> dict:
    keys = jax.random.split(jax.random.key(seed), 6)
    points = scatter_about(keys[0], (NPTS, D), 1.0, 6.0, ((0, 512),))
    candidates_keys = jax.random.split(jax.random.fold_in(keys[1], 1), NPTS // PTS_DEV)
    candidates_turns = jax.random.permutation(jax.random.fold_in(keys[1], 3), NPTS // PTS_DEV)
    candidates = jax.vmap(lambda own, number: deal_out(jax.random.fold_in(keys[1], 2), own, number, PTS_DEV, NBLK, CANDS, CAP, 2))(candidates_keys, candidates_turns).reshape((NPTS, CANDS))
    means = scatter_about(keys[2], (K, D), 0.05, 0.75, ((0, 16),))
    variances = jnp.clip(1.0 + 0.02 * jax.random.normal(keys[3], (K,), jnp.float32), 0.9, 1.1)
    log_weights = scatter_about(keys[4], (K,), 1.0, 4.0, ((0, 16),), jnp.float32)
    return {"points": points, "candidates": candidates, "means": means, "variances": variances, "log_weights": log_weights}


def log_density(rows, mu, var, logw):
    rows32 = rows.astype(jnp.float32)
    mu32 = mu.astype(jnp.float32)
    inner = jnp.dot(rows32, mu32.T, precision=lax.Precision.HIGHEST)
    xx = jnp.sum(rows32 * rows32, axis=1)
    mm = jnp.sum(mu32 * mu32, axis=1)
    const = logw - 0.5 * D * jnp.log(2.0 * math.pi * var)
    return const[None, :] - (xx[:, None] - 2.0 * inner + mm[None, :]) / (2.0 * var[None, :]), xx


def reference(points, candidates, means, variances, log_weights):
    npair = NPTS * CANDS
    padb = CAP * N_PTS * N_COMP
    flat = candidates.reshape(-1)
    seq = jnp.arange(npair, dtype=jnp.int32)
    order = jnp.argsort(flat * npair + seq).astype(jnp.int32)
    counts_blk = jnp.sum((flat[:, None] == jnp.arange(NBLK, dtype=jnp.int32)[None, :]).astype(jnp.int32), axis=0)
    starts = (jnp.cumsum(counts_blk) - counts_blk).astype(jnp.int32)
    order_pad = jnp.concatenate([order, jnp.full((padb,), npair, jnp.int32)])

    def block_data(b):
        idx = lax.dynamic_slice_in_dim(order_pad, starts[b], padb)
        valid = jnp.arange(padb, dtype=jnp.int32) < counts_blk[b]
        pair = jnp.where(valid, idx, 0).astype(jnp.int32)
        rows = points[pair // CANDS]
        mu = lax.dynamic_slice_in_dim(means, b * BLOCK, BLOCK)
        var = lax.dynamic_slice_in_dim(variances, b * BLOCK, BLOCK)
        logw = lax.dynamic_slice_in_dim(log_weights, b * BLOCK, BLOCK)
        logp, xx = log_density(rows, mu, var, logw)
        return pair, valid, rows, logp, xx

    def first(b):
        pair, valid, rows, logp, xx = block_data(b)
        bmax = jnp.max(logp, axis=1)
        bsum = jnp.sum(jnp.exp(logp - bmax[:, None]), axis=1)
        return jnp.where(valid, pair, npair), bmax, bsum

    blocks = jnp.arange(NBLK, dtype=jnp.int32)
    target, bmax, bsum = lax.map(first, blocks)
    target = target.reshape(-1)
    pmax = jnp.zeros((npair + 1,), jnp.float32).at[target].set(bmax.reshape(-1))[:npair].reshape(NPTS, CANDS)
    psum = jnp.zeros((npair + 1,), jnp.float32).at[target].set(bsum.reshape(-1))[:npair].reshape(NPTS, CANDS)
    top = jnp.max(pmax, axis=1)
    loglik = top + jnp.log(jnp.sum(psum * jnp.exp(pmax - top[:, None]), axis=1))

    def second(b):
        pair, valid, rows, logp, xx = block_data(b)
        resp = jnp.exp(logp - loglik[pair // CANDS][:, None])
        resp = jnp.where(valid[:, None], resp, 0.0)
        counts = jnp.sum(resp, axis=0)
        sqsum = jnp.sum(resp * xx[:, None], axis=0)
        resp16 = resp.astype(jnp.bfloat16).astype(jnp.float32)
        wsum = jnp.dot(resp16.T, rows.astype(jnp.float32), precision=lax.Precision.HIGHEST)
        return counts, sqsum, wsum

    counts, sqsum, wsum = lax.map(second, blocks)
    counts = counts.reshape(K)
    sqsum = sqsum.reshape(K)
    wsum = wsum.reshape(K, D)
    mu_old = means.astype(jnp.float32)
    new_means = (wsum + mu_old) / (counts + 1.0)[:, None]
    resid = sqsum - 2.0 * jnp.sum(new_means * wsum, axis=1) + counts * jnp.sum(new_means * new_means, axis=1) + D * variances
    new_variances = resid / (D * (counts + 1.0))
    new_log_weights = jnp.log((counts + 1.0) / float(NPTS + K))
    return loglik, new_means.reshape(N_COMP, KDEV, D), new_variances.reshape(N_COMP, KDEV), new_log_weights.reshape(N_COMP, KDEV)
```

```python
import math

import jax
import jax.numpy as jnp
from jax import lax
from jax.sharding import PartitionSpec as P

LOW = -1e30


def split3(v):
    hi = lax.reduce_precision(v, 8, 7)
    mid = lax.reduce_precision(v - hi, 8, 7)
    lo = v - hi - mid
    return [hi, mid, lo]


def make_body(npts, ncomp, nx):
    nz = npts // nx
    ny = ncomp // 2
    clockwise = [(c, (c + 2) % ncomp) for c in range(ncomp)]
    counter = [(c, (c - 2) % ncomp) for c in range(ncomp)]
    partner = [(c, c ^ 1) for c in range(ncomp)]
    same_core = [[2 * y + core for y in range(ny)] for core in range(2)]
    along_x = [[z * nx + x for x in range(nx)] for z in range(nz)]
    along_z = [[z * nx + x for z in range(nz)] for x in range(nx)]

    def on_device(points, candidates, means, variances, log_weights):
        rows, width = points.shape
        owned = means.shape[0]
        block = owned // 2
        share = owned // npts
        me = lax.axis_index("comp")
        my_y = me // 2
        f32 = jnp.float32
        bf16 = jnp.bfloat16

        chunks = [None] * ny
        chunks[0] = points
        up = down = points
        for step in range(1, ny // 2):
            up = lax.ppermute(up, "comp", clockwise)
            down = lax.ppermute(down, "comp", counter)
            chunks[step] = up
            chunks[ny - step] = down
        half = rows // 2
        top_half = lax.ppermute(up[:half], "comp", clockwise)
        low_half = lax.ppermute(down[half:], "comp", counter)
        chunks[ny // 2] = jnp.concatenate([top_half, low_half], axis=0)

        def regroup(v):
            tail = v.shape[1:]
            order = (1, 0, 2) + tuple(range(3, 3 + len(tail)))
            return v.reshape((nz, nx, share) + tail).transpose(order).reshape(v.shape)

        my_means = regroup(means)
        their_means = lax.ppermute(my_means, "comp", partner)
        mu = jnp.concatenate([my_means, their_means], axis=0)
        small = jnp.stack([regroup(variances), regroup(log_weights)])
        small = jnp.concatenate([small, lax.ppermute(small, "comp", partner)], axis=1)
        var, logw = small[0], small[1]
        mm = jnp.sum(mu.astype(f32) ** 2, axis=1)
        const = logw - 0.5 * width * jnp.log(2.0 * math.pi * var)
        local_block = regroup(jnp.arange(owned, dtype=jnp.int32) // block)
        block_of = jnp.concatenate([2 * me + local_block, 2 * (me ^ 1) + local_block])

        cand_all = lax.all_to_all(
            jnp.broadcast_to(candidates[None], (ny,) + candidates.shape),
            "comp",
            split_axis=0,
            concat_axis=0,
            axis_index_groups=same_core,
            tiled=True,
        )

        logps, lses, xxs = [], [], []
        for r in range(ny):
            x = chunks[r]
            cand = lax.dynamic_index_in_dim(cand_all, (my_y - r) % ny, 0, keepdims=False)
            inner = lax.dot_general(x, mu, (((1,), (1,)), ((), ())), preferred_element_type=f32)
            xx = jnp.sum(x.astype(f32) ** 2, axis=1)
            logp = const[None, :] - (xx[:, None] - 2.0 * inner + mm[None, :]) / (2.0 * var[None, :])
            named = cand[:, 0:1] == block_of[None, :]
            for i in range(1, candidates.shape[1]):
                named = named | (cand[:, i : i + 1] == block_of[None, :])
            logp = jnp.where(named, logp, LOW)
            top = jnp.max(logp, axis=1)
            lses.append(top + jnp.log(jnp.sum(jnp.exp(logp - top[:, None]), axis=1)))
            logps.append(logp)
            xxs.append(xx)

        lse = jnp.stack(lses)
        source = (my_y - jnp.arange(ny, dtype=jnp.int32)) % ny
        match = source[:, None] == jnp.arange(ny, dtype=jnp.int32)[None, :]
        lse_abs = jnp.sum(jnp.where(match[:, :, None], lse[:, None, :], 0.0), axis=0)
        shared = lax.all_to_all(
            jnp.broadcast_to(lse_abs.reshape(1, ny * rows), (ny, ny * rows)),
            "comp",
            split_axis=0,
            concat_axis=0,
            axis_index_groups=same_core,
            tiled=True,
        )
        peak = jnp.max(shared, axis=0)
        total = (peak + jnp.log(jnp.sum(jnp.exp(shared - peak[None]), axis=0))).reshape(ny, rows)
        total_rel = jnp.sum(jnp.where(match[:, :, None], total[None], 0.0), axis=1)
        loglik = total_rel[0]

        logp = jnp.concatenate(logps, axis=0)
        xx = jnp.concatenate(xxs, axis=0)
        x_all = jnp.concatenate(chunks, axis=0)
        resp = jnp.exp(logp - total_rel.reshape(-1)[:, None])
        counts = jnp.sum(resp, axis=0)
        sqsum = jnp.sum(resp * xx[:, None], axis=0)
        resp16 = resp.astype(bf16)

        def summed(part):
            return lax.dot_general(part, x_all, (((0,), (0,)), ((), ())), preferred_element_type=f32)

        def packed(w, c, s):
            extra = jnp.stack(split3(c) + split3(s), axis=1)
            extra = jnp.pad(extra, ((0, 0), (0, 128 - extra.shape[1])))
            return jnp.concatenate([w.astype(bf16), extra.astype(bf16)], axis=1)

        def unpacked(total):
            w = total[:, :width]
            c = total[:, width] + total[:, width + 1] + total[:, width + 2]
            s = total[:, width + 3] + total[:, width + 4] + total[:, width + 5]
            return w, c, s

        theirs = packed(summed(resp16[:, owned:]), counts[owned:], sqsum[owned:])
        from_partner = lax.ppermute(theirs, "comp", partner)
        mine = summed(resp16[:, :owned])
        w, c, s = unpacked(from_partner.astype(f32))
        out = packed(mine + w, counts[:owned] + c, sqsum[:owned] + s)

        got = lax.all_to_all(
            out, "pts", split_axis=0, concat_axis=0, axis_index_groups=along_x, tiled=True
        ).reshape(nx, owned // nx, width + 128)
        w, c, s = unpacked(jnp.sum(got.astype(f32), axis=0))
        got = lax.all_to_all(
            packed(w, c, s), "pts", split_axis=0, concat_axis=0, axis_index_groups=along_z, tiled=True
        ).reshape(nz, share, width + 128)
        wsum_own, counts_own, sqsum_own = unpacked(jnp.sum(got.astype(f32), axis=0))

        first_row = lax.axis_index("pts") * share
        mu_old = lax.dynamic_slice_in_dim(means, first_row, share, 0).astype(f32)
        var_old = lax.dynamic_slice_in_dim(variances, first_row, share, 0)
        new_means = (wsum_own + mu_old) / (counts_own + 1.0)[:, None]
        resid = (
            sqsum_own
            - 2.0 * jnp.sum(new_means * wsum_own, axis=1)
            + counts_own * jnp.sum(new_means * new_means, axis=1)
            + width * var_old
        )
        new_variances = resid / (width * (counts_own + 1.0))
        total_points = rows * ncomp * npts
        new_log_weights = jnp.log((counts_own + 1.0) / float(total_points + owned * ncomp))
        return (
            loglik,
            new_means.reshape(1, share, width),
            new_variances.reshape(1, share),
            new_log_weights.reshape(1, share),
        )

    return on_device


def solution(mesh):
    return jax.shard_map(
        make_body(mesh.shape["pts"], mesh.shape["comp"], 4),
        mesh=mesh,
        in_specs=(
            P(("pts", "comp"), None),
            P(("pts", "comp"), None),
            P("comp", None),
            P("comp"),
            P("comp"),
        ),
        out_specs=(P(("pts", "comp")), P("comp", "pts", None), P("comp", "pts"), P("comp", "pts")),
        check_vma=False,
    )
```
